128 devices in a mesh: tx: 8 (over x, core), ty: 16 (over z, y).
Axes of the slice: x: 4, y: 4, z: 4, core: 2. Of those that a mesh axis runs over, the one named last changes fastest.
Arguments:
- solution: float32 [4, 1024, 4096], P(None, 'tx', 'ty'), may hold values from -6 to 6
- residual: float32 [4, 1024, 4096], P(None, 'tx', 'ty')
- direction: float32 [4, 1024, 4096], P(None, 'tx', 'ty')
- blocks: bfloat16 [32768, 128, 256], P(('tx', 'ty')), may hold values from -0.375 to 0.375
- bin_owner: int32 [32768, 1], P(('tx', 'ty')), may hold values from 0 to 127; in each aligned block of 256 rows (0 to 255, 256 to 511, ...) at most 3 rows name the same one
- bin_tile: int32 [32768], P(('tx', 'ty')), may hold values from 0 to 127
Outputs:
- next_solution: float32 [4, 1024, 4096], P(None, 'tx', 'ty')
- next_residual: float32 [4, 1024, 4096], P(None, 'tx', 'ty')
- next_direction: float32 [4, 1024, 4096], P(None, 'tx', 'ty')
The draws below stay inside these ranges and needn't reach their ends.
Inputs may be any that keep to these rules, and one draw needn't show every extreme that they name: `bin_owner`: among the bins of one device, at most 3 name the same owner, and on some devices some owner is named by exactly 3 of them.
All inputs are finite; a program needn't handle non-finite values.
Results may differ from the reference program's by a relative error of at most 0.0024.
Values may be sent and summed in bfloat16 or wider, within the bound.
A program may use at most 128 MiB of HBM per device.

```python
import math
import jax
import jax.numpy as jnp
import numpy as np
from jax import lax

BEACONS = 4
TILE_SIDE = 16
TILE_CELLS = 256
BIN_ROWS = 128
ROWS_DEV = 128
COLS_DEV = 256
BINS_DEV = 256
CAP = 3
TILES_DEV = 128
ROWS = 1024
COLS = 4096
BINS = 32768
N_TX = 8
N_TY = 16


def rough_field(key):
    keys = jax.random.split(key, 2)
    rows = jnp.arange(ROWS, dtype=jnp.float32)[:, None] / ROWS
    cols = jnp.arange(COLS, dtype=jnp.float32)[None, :] / COLS
    slope = jnp.exp(math.log(3.0) * (rows + cols)) / 3.0
    beacon = jax.random.uniform(keys[0], (BEACONS, 1, 1), minval=0.5, maxval=2.0)
    scale = slope[None, :, :] * beacon
    noise = jax.random.normal(keys[1], (BEACONS, ROWS, COLS), dtype=jnp.float32)
    return (scale * noise).astype(jnp.float32)


def draw_residual(key, part):
    return rough_field(jax.random.fold_in(key, 11))


def draw_direction(key, part):
    return rough_field(jax.random.fold_in(key, 23))


def set_ends(entries, rng, low, high):
    dims = entries.shape
    index_at = [jax.random.randint(jax.random.fold_in(rng, axis), (), 0, dims[axis]) for axis in range(len(dims))]
    entries = entries.at[tuple(index_at)].set(low)
    longest = dims.index(max(dims))
    index_at[longest] = (index_at[longest] + 1) % dims[longest]
    return entries.at[tuple(index_at)].set(high)


def shard_levels(stream_key, shape, cuts, least, high):
    loudness = 1.0
    for dim, blocks in cuts:
        heights = jax.random.uniform(jax.random.fold_in(jax.random.fold_in(stream_key, 6), dim), (blocks,), jnp.float32, least / len(cuts), high / len(cuts))
        loudness = loudness * jnp.repeat(jnp.exp(heights), shape[dim] // blocks).reshape((-1,) + (1,) * (len(shape) - 1 - dim))
    return loudness


def deal_out(own_key, own, number, rows, count, top, most, skew):
    ranking = jax.random.permutation(own_key, count)
    heavy_load, usual = load_shares(count, rows * top, most, skew, True), load_shares(count, rows * top, most, skew, False)
    places = jnp.arange(count)

    def named(sizes, offset_by):
        used = int((sizes > 0).sum())
        fixed = max(1, used // 4)
        passed = fixed + (places - fixed + offset_by * (used - fixed)) % max(1, count - fixed)
        return jnp.zeros((count,), jnp.int32).at[ranking[jnp.where(places < fixed, places, passed)]].set(jnp.asarray(sizes, jnp.int32))

    sizes = jnp.where(number % 4 == 0, named(heavy_load, number // 4), named(usual, number - number // 4 - 1))
    mixed = jax.random.permutation(jax.random.fold_in(own, 3), count)
    donor, sink = mixed[0:count // 2 * 2:2], mixed[1:count // 2 * 2:2]
    room = jnp.minimum(sizes[donor] - 1, most - sizes[sink]) // 2
    room = jnp.where((donor == ranking[0]) | (sink == ranking[0]) | (sizes[sink] == 0), 0, jnp.maximum(room, 0))
    passed = jax.random.randint(jax.random.fold_in(own, 4), (count // 2,), 0, 1 << 20) % (room + 1)
    sizes = sizes.at[donor].add(-passed).at[sink].add(passed)
    labels = jnp.searchsorted(jnp.cumsum(sizes), jnp.arange(rows * top), side="right").astype(jnp.int32)
    listing = labels.reshape(top, rows).T
    listing = listing[jax.random.permutation(jax.random.fold_in(own, 1), rows)]
    offset_by = jax.random.randint(jax.random.fold_in(own, 2), (rows, 1), 0, top)
    return jnp.take_along_axis(listing, (jnp.arange(top)[None, :] + offset_by) % top, axis=1)


def load_shares(number_of, total, bound, skew, full):
    portions = [(1 << 20) // math.isqrt(standing ** skew) + 1 for standing in range(1, number_of + 1)]
    largest = bound if full else min(bound, max(-(-total // number_of), total * portions[0] // sum(portions)))
    least = 1 if total - largest >= number_of - 1 else 0
    counts, surplus = [largest] + [least] * (number_of - 1), total - largest - least * (number_of - 1)
    while surplus > 0:
        candidates = [i for i in range(1, number_of) if counts[i] < largest] or [i for i in range(1, number_of) if counts[i] < bound]
        mass, left = sum([portions[i] for i in candidates]), surplus
        for i in candidates:
            more = min(bound - counts[i], max(1, left * portions[i] // mass), surplus)
            counts[i] = counts[i] + more
            surplus = surplus - more
    return np.array(counts)


def bell_draw(rng, dims, scale, bound, cuts=(), kind=jnp.bfloat16):
    values = scale * jax.random.normal(rng, dims, jnp.float32)
    if cuts:
        values = values * shard_levels(rng, dims, cuts, -0.22, 0.18)
    return jnp.clip(values, -bound, bound).astype(kind)


def setup_inputs(seed: int = 0) -> dict:
    arg_keys = jax.random.split(jax.random.key(seed), 7)
    solution = bell_draw(arg_keys[0], (BEACONS, ROWS, COLS), 1.0, 6.0, ((1, 8), (2, 16)), jnp.float32)
    residual = draw_residual(jax.random.fold_in(arg_keys[6], 71), 0)
    direction = draw_direction(jax.random.fold_in(arg_keys[6], 71), 0)
    blocks = bell_draw(arg_keys[3], (BINS, BIN_ROWS, TILE_CELLS), TILE_CELLS ** -0.5, 0.375, ((0, 128),))
    bin_owner_keys = jax.random.split(jax.random.fold_in(arg_keys[4], 1), BINS // BINS_DEV)
    bin_owner_turns = jax.random.permutation(jax.random.fold_in(arg_keys[4], 3), BINS // BINS_DEV)
    bin_owner = jax.vmap(lambda own, number: deal_out(jax.random.fold_in(arg_keys[4], 2), own, number, BINS_DEV, N_TX * N_TY, 1, CAP, 2))(bin_owner_keys, bin_owner_turns).reshape((BINS, 1))
    bin_tile = set_ends(jax.random.randint(arg_keys[5], (BINS,), 0, TILES_DEV), jax.random.fold_in(arg_keys[5], 1), 0, TILES_DEV - 1).astype(jnp.int32)
    return dict(solution=solution, residual=residual, direction=direction, blocks=blocks, bin_owner=bin_owner, bin_tile=bin_tile)


smooth_weight = 0.25


def laplace(field):
    padded = jnp.pad(field, ((0, 0), (1, 1), (1, 1)))
    near = padded[:, 2:, 1:-1] + padded[:, :-2, 1:-1] + padded[:, 1:-1, 2:] + padded[:, 1:-1, :-2]
    return 4.0 * field - near


def split_tiles(field):
    across = ROWS_DEV // TILE_SIDE
    down = COLS_DEV // TILE_SIDE
    shaped = field.reshape(BEACONS, N_TX, across, TILE_SIDE, N_TY, down, TILE_SIDE)
    shaped = shaped.transpose(1, 4, 2, 5, 0, 3, 6)
    return shaped.reshape(N_TX * N_TY * across * down, BEACONS, TILE_SIDE * TILE_SIDE)


def join_tiles(tiles):
    across = ROWS_DEV // TILE_SIDE
    down = COLS_DEV // TILE_SIDE
    shaped = tiles.reshape(N_TX, N_TY, across, down, BEACONS, TILE_SIDE, TILE_SIDE)
    shaped = shaped.transpose(4, 0, 2, 5, 1, 3, 6)
    return shaped.reshape(BEACONS, ROWS_DEV * N_TX, COLS_DEV * N_TY)


def reference(solution, residual, direction, blocks, bin_owner, bin_tile):
    devices = N_TX * N_TY
    tiles_dev = (ROWS_DEV // TILE_SIDE) * (COLS_DEV // TILE_SIDE)
    rounded = split_tiles(direction.astype(jnp.bfloat16))
    places = (bin_owner[:, 0] * tiles_dev + bin_tile).astype(jnp.int32)
    weights = blocks.reshape(devices, BINS_DEV, BIN_ROWS, TILE_CELLS)
    places = places.reshape(devices, BINS_DEV)

    def add_device(total, item):
        block, rows_at = item
        picked = rounded[rows_at].astype(jnp.float32)
        wide = block.astype(jnp.float32)
        samples = jnp.einsum("bsc,bkc->bks", wide, picked).astype(jnp.bfloat16)
        adjoint = jnp.einsum("bsc,bks->bkc", wide, samples.astype(jnp.float32))
        return total.at[rows_at].add(adjoint), None

    total, _ = lax.scan(add_device, jnp.zeros(rounded.shape, jnp.float32), (weights, places))
    image = join_tiles(total) + smooth_weight * laplace(direction)
    norm_old = jnp.sum(residual * residual, axis=(1, 2))
    curvature = jnp.sum(direction * image, axis=(1, 2))
    alpha = (norm_old / curvature)[:, None, None]
    next_solution = solution + alpha * direction
    next_residual = residual - alpha * image
    norm_new = jnp.sum(next_residual * next_residual, axis=(1, 2))
    next_direction = next_residual + (norm_new / norm_old)[:, None, None] * direction
    return next_solution, next_residual, next_direction
```

```python
import functools

import jax
import jax.numpy as jnp
from jax import lax
from jax.experimental import pallas as pl
from jax.experimental.pallas import tpu as pltpu
from jax.sharding import PartitionSpec as P

MESH = pl.DeviceIdType.MESH
SIDE = 16
CELLS = 256
SLOTS = 3
GROUP = 16
F32 = jnp.float32
BF16 = jnp.bfloat16
smooth_weight = 0.25


def iota(shape, dim):
    return lax.broadcasted_iota(jnp.int32, shape, dim)


def nt_dot(a, b):
    return lax.dot_general(a, b, (((1,), (1,)), ((), ())), preferred_element_type=F32)


def dot(a, b):
    return jnp.dot(a, b, preferred_element_type=F32)


def swap_chunks(load_row, groups, lhs, rep, parts, write):
    rows = groups * SIDE
    keep = iota((rows, CELLS), 0) % SIDE == iota((rows, CELLS), 1) // SIDE
    for part in range(parts):
        for b in range(SIDE):
            row = load_row(b, part)
            wide = jnp.broadcast_to(row, (groups, SIDE, CELLS)).reshape(rows, CELLS)
            lhs[:, b * CELLS : (b + 1) * CELLS] = jnp.where(keep, wide, 0.0).astype(BF16)
        step = rows // 4

        def body(i, _):
            at = pl.ds(pl.multiple_of(i * step, step), step)
            write(part, i, at, dot(lhs[at, :], rep[...]))
            return 0

        lax.fori_loop(0, 4, body, 0)


def kernel(
    nx, ny, owner_ref, tile_ref, dir_hbm, res_hbm, blocks_hbm,
    img_ref, coef_ref,
    dirv, resv, blk, rep, lhs, tiles, req, reqr, table, slots, bits, turned,
    out, rcv, ret, retr, data, low, halo, halor, row, rowr,
    load_sem, blk_sem, slot_sem, req_sem, halo_sem, halor_sem,
    fetch_sem, fetchr_sem, back_sem, backr_sem, sum_sem,
):
    n = nx * ny
    groups = n // GROUP
    count = blk.shape[0]
    tx, ty = lax.axis_index("tx"), lax.axis_index("ty")
    me = tx * ny + ty

    def ahead(d):
        peer = (me + d) % n
        return (peer // ny, peer % ny)

    def behind(d):
        peer = (me + n - d) % n
        return (peer // ny, peer % ny)

    load_dir = pltpu.make_async_copy(dir_hbm, dirv, load_sem.at[0])
    load_dir.start()
    load_res = pltpu.make_async_copy(res_hbm, resv, load_sem.at[1])
    load_blk = pltpu.make_async_copy(blocks_hbm, blk, blk_sem)
    load_blk.start()
    load_res.start()

    barrier = pltpu.get_barrier_semaphore()

    def greet(d, _):
        pl.semaphore_signal(barrier, inc=1, device_id=ahead(d), device_id_type=MESH)
        return 0

    lax.fori_loop(1, n, greet, 0)

    away = (owner_ref[...] - me + n) % n
    member = jnp.broadcast_to(away, (n, count)) == iota((n, count), 0)
    earlier = (iota((count, count), 0) < iota((count, count), 1)).astype(F32).astype(BF16)
    rank = dot(member.astype(F32).astype(BF16), earlier)
    coded = jnp.where(member, jnp.where(rank == 0.0, 1.0, jnp.where(rank == 1.0, 2.0, 4.0)), 0.0)
    named = (jnp.broadcast_to(tile_ref[...], (n, count)) == iota((n, count), 0)).astype(F32).astype(BF16)
    asked = nt_dot(coded.astype(BF16), named).astype(jnp.int32)
    req[...] = asked.reshape(n, 1, n)
    number = iota((8, count), 1).astype(F32).astype(BF16)
    bins = jnp.zeros((8, n), F32)
    for s in range(SLOTS):
        pick = jnp.where(member & (rank == float(s)), 1.0, 0.0).astype(BF16)
        bins = jnp.where(iota((8, n), 0) == s, nt_dot(number, pick), bins)
    table[...] = bins.astype(jnp.int32)
    same = iota((CELLS, CELLS), 0) % SIDE == iota((CELLS, CELLS), 1) % SIDE
    for b in range(SIDE):
        here = same & (iota((CELLS, CELLS), 1) // SIDE == b)
        rep[b * CELLS : (b + 1) * CELLS, :] = here.astype(F32).astype(BF16)

    load_dir.wait()
    beacons, rows, cols = dirv.shape
    edge_lane = jnp.where(iota((8, cols), 0) == 0, cols - 1, 0)
    edge = ((iota((8, cols), 1) == edge_lane) & (iota((8, cols), 0) < 2)).astype(F32).astype(BF16)
    for k in range(beacons):
        halo[0, k : k + 1, :] = dirv[k, rows - 1 : rows, :]
        halo[1, k : k + 1, :] = dirv[k, 0:1, :]
        ends = nt_dot(edge, dirv[k].astype(BF16))
        halo[2, k : k + 1, :rows] = ends[0:1, :]
        halo[3, k : k + 1, :rows] = ends[1:2, :]

    pl.semaphore_wait(barrier, n - 1)

    def ask(d, _):
        pltpu.make_async_remote_copy(
            req.at[d], reqr.at[d], req_sem.at[0], req_sem.at[1], device_id=ahead(d), device_id_type=MESH
        ).start()
        return 0

    lax.fori_loop(1, n, ask, 0)
    reqr[0] = req[0]
    sides = (((tx + 1) % nx, ty), ((tx + nx - 1) % nx, ty), (tx, (ty + 1) % ny), (tx, (ty + ny - 1) % ny))
    edges = [
        pltpu.make_async_remote_copy(
            halo.at[i], halor.at[i], halo_sem.at[i], halor_sem.at[i], device_id=side, device_id_type=MESH
        )
        for i, side in enumerate(sides)
    ]
    for copy in edges:
        copy.start()
    to_scalar = pltpu.make_async_copy(table, slots, slot_sem)
    to_scalar.start()

    def direction_row(b, part):
        return dirv[...].reshape(beacons * rows // SIDE, SIDE, cols)[:, b : b + 1, :]

    def write_tiles(part, i, at, value):
        tiles[at, :] = value.astype(BF16)

    swap_chunks(direction_row, beacons * rows // SIDE, lhs, rep, 1, write_tiles)

    rest = pl.ds(1, n - 1)
    asking = pltpu.make_async_remote_copy(
        req.at[rest], reqr.at[rest], req_sem.at[0], req_sem.at[1], device_id=ahead(1), device_id_type=MESH
    )
    asking.wait_recv()

    slot_rows = GROUP * SIDE
    at_slot = iota((slot_rows, n), 0) % SIDE // beacons
    at_beacon = iota((slot_rows, n), 0) % beacons

    def fetch_copy(d):
        return pltpu.make_async_remote_copy(
            out.at[d], rcv.at[d], fetch_sem, fetchr_sem.at[d // GROUP], device_id=behind(d), device_id_type=MESH
        )

    def send_fetch(d, _):
        fetch_copy(d).start()
        return 0

    def serve(g, _):
        span = pl.ds(g * GROUP, GROUP)
        words = jnp.broadcast_to(reqr[span], (GROUP, SIDE, n)).reshape(slot_rows, n)
        bit = (lax.shift_right_logical(words, at_slot) & 1).astype(F32)
        bits[pl.ds(pl.multiple_of(g * slot_rows, slot_rows), slot_rows), :] = bit
        pick = jnp.concatenate(
            [jnp.where(at_beacon == k, bit, 0.0).astype(BF16) for k in range(beacons)], axis=1
        )
        out[span] = dot(pick, tiles[...]).astype(BF16).reshape(GROUP, SIDE, CELLS)

        @pl.when(g > 0)
        def _():
            lax.fori_loop(jnp.maximum((g - 1) * GROUP, 1), g * GROUP, send_fetch, 0)

        return 0

    lax.fori_loop(0, groups, serve, 0)
    rcv[0] = out[0]
    lax.fori_loop((groups - 1) * GROUP, n, send_fetch, 0)

    lane_beacon = iota((n, slot_rows), 1) % beacons

    def turn(g, _):
        span = pl.ds(pl.multiple_of(g * slot_rows, slot_rows), slot_rows)
        flipped = jnp.transpose(bits[span, :])
        for k in range(beacons):
            turned[g, k * n : (k + 1) * n, :] = jnp.where(lane_beacon == k, flipped, 0.0).astype(BF16)
        return 0

    lax.fori_loop(0, groups, turn, 0)

    to_scalar.wait()
    load_blk.wait()
    row_slot = iota((SIDE, rows), 0) // beacons

    def back_copy(d):
        return pltpu.make_async_remote_copy(
            ret.at[d], retr.at[d], back_sem, backr_sem.at[d // GROUP], device_id=ahead(d), device_id_type=MESH
        )

    def send_back(d, _):
        back_copy(d).start()
        return 0

    def bin_work(d):
        x = rcv[d]
        total = jnp.zeros((SIDE, CELLS), F32)
        for s in range(SLOTS):
            block = blk[jnp.clip(slots[s, d], 0, count - 1)]
            sample = nt_dot(x, block)
            sample = jnp.where(row_slot == s, sample, 0.0).astype(BF16)
            total = total + dot(sample, block)
        ret[d] = total.astype(BF16)

    for g in range(groups):
        first = g * GROUP + (1 if g == 0 else 0)
        span = pl.ds(first, (g + 1) * GROUP - first)
        pltpu.make_async_remote_copy(
            out.at[span], rcv.at[span], fetch_sem, fetchr_sem.at[g], device_id=behind(1), device_id_type=MESH
        ).wait_recv()

        def four(i, _):
            for u in range(4):
                bin_work(g * GROUP + i * 4 + u)
            return 0

        lax.fori_loop(0, GROUP // 4, four, 0)
        if g > 0:
            lax.fori_loop(max((g - 1) * GROUP, 1), g * GROUP, send_back, 0)
    retr[0] = ret[0]
    lax.fori_loop((groups - 1) * GROUP, n, send_back, 0)

    load_res.wait()
    for copy in edges:
        copy.wait()
    row_at, lane_at = iota((rows, cols), 0), iota((rows, cols), 1)
    diagonal = iota((rows, rows), 0) == iota((rows, rows), 1)
    spread = iota((2 * rows, cols), 0) // rows == iota((2 * rows, cols), 1) // (cols - 1)
    spread = spread & ((iota((2 * rows, cols), 1) == 0) | (iota((2 * rows, cols), 1) == cols - 1))
    spread = spread.astype(F32).astype(BF16)
    for k in range(beacons):
        field = dirv[k]
        above = jnp.where(tx > 0, halor[0, k : k + 1, :], 0.0)
        below = jnp.where(tx < nx - 1, halor[1, k : k + 1, :], 0.0)
        left = jnp.where(ty > 0, halor[2, k : k + 1, :rows], 0.0)
        right = jnp.where(ty < ny - 1, halor[3, k : k + 1, :rows], 0.0)
        ends = jnp.concatenate(
            [jnp.where(diagonal, left, 0.0).astype(BF16), jnp.where(diagonal, right, 0.0).astype(BF16)], axis=1
        )
        near = dot(ends, spread)
        near = near + jnp.where(row_at == 0, above, pltpu.roll(field, 1, 0))
        near = near + jnp.where(row_at == rows - 1, below, pltpu.roll(field, rows - 1, 0))
        near = near + jnp.where(lane_at == 0, 0.0, pltpu.roll(field, 1, 1))
        near = near + jnp.where(lane_at == cols - 1, 0.0, pltpu.roll(field, cols - 1, 1))
        img_ref[k] = smooth_weight * (4.0 * field - near)

    for g in range(groups):
        first = g * GROUP + (1 if g == 0 else 0)
        span = pl.ds(first, (g + 1) * GROUP - first)
        pltpu.make_async_remote_copy(
            ret.at[span], retr.at[span], back_sem, backr_sem.at[g], device_id=ahead(1), device_id_type=MESH
        ).wait_recv()
        part = dot(turned[g], retr[g * GROUP : (g + 1) * GROUP].reshape(slot_rows, CELLS))
        if g == 0:
            data[...] = part
        else:
            data[...] += part

    value = data[...]
    low[...] = value - value.astype(BF16).astype(F32)

    def data_row(b, part):
        source = data if part == 0 else low
        return source[...].reshape(beacons * rows // SIDE, SIDE, cols)[:, b : b + 1, :]

    def write_image(part, i, at, value):
        img_ref[i] = img_ref[i] + value

    swap_chunks(data_row, beacons * rows // SIDE, lhs, rep, 2, write_image)

    lane = iota((1, n), 1)
    line = jnp.zeros((1, n), F32)
    for k in range(beacons):
        image, field, old = img_ref[k], dirv[k], resv[k]
        top = jnp.maximum(jnp.max(jnp.abs(image), axis=(0, 1), keepdims=True), 1e-30)
        scaled = image * (1.0 / top)
        facts = (
            jnp.sum(old * old, axis=(0, 1), keepdims=True),
            jnp.sum(field * image, axis=(0, 1), keepdims=True),
            top,
            jnp.sum(old * scaled, axis=(0, 1), keepdims=True),
            jnp.sum(scaled * scaled, axis=(0, 1), keepdims=True),
        )
        for q, fact in enumerate(facts):
            line = jnp.where(lane == q * beacons + k, fact, line)
    row[0] = line
    rowr[0] = line

    def tell(d, _):
        pltpu.make_async_remote_copy(
            row.at[0], rowr.at[d], sum_sem.at[0], sum_sem.at[1], device_id=ahead(d), device_id_type=MESH
        ).start()
        return 0

    lax.fori_loop(1, n, tell, 0)

    asking.wait_send()
    for phase, sem in ((out, fetch_sem), (ret, back_sem)):
        pltpu.make_async_remote_copy(
            phase.at[rest], phase.at[rest], sem, sem, device_id=ahead(1), device_id_type=MESH
        ).wait_send()
    telling = pltpu.make_async_remote_copy(
        rowr.at[rest], rowr.at[rest], sum_sem.at[0], sum_sem.at[1], device_id=ahead(1), device_id_type=MESH
    )
    telling.wait_recv()
    lines = rowr[...].reshape(n, n)
    sums = jnp.sum(lines, axis=0, keepdims=True)
    alpha = sums / pltpu.roll(sums, n - beacons, 1)
    reach = alpha * pltpu.roll(lines, n - 2 * beacons, 1)
    cross = pltpu.roll(lines, n - 3 * beacons, 1)
    square = pltpu.roll(lines, n - 4 * beacons, 1)
    after = jnp.sum(lines - 2.0 * reach * cross + reach * reach * square, axis=0, keepdims=True)
    beta = after / sums
    coef_ref[...] = jnp.where(iota((8, n), 0) == 0, alpha, beta)
    telling.wait_send()


def per_device(nx, ny, solution, residual, direction, blocks, bin_owner, bin_tile):
    beacons, rows, cols = direction.shape
    count = blocks.shape[0]
    n = nx * ny
    groups = n // GROUP
    anyspace = pl.BlockSpec(memory_space=pl.ANY)
    vmem = pl.BlockSpec(memory_space=pltpu.VMEM)
    dma = pltpu.SemaphoreType.DMA
    image, coef = pl.pallas_call(
        functools.partial(kernel, nx, ny),
        out_shape=(
            jax.ShapeDtypeStruct((beacons, rows, cols), F32),
            jax.ShapeDtypeStruct((8, n), F32),
        ),
        in_specs=[vmem, vmem, anyspace, anyspace, anyspace],
        out_specs=(vmem, vmem),
        scratch_shapes=[
            pltpu.VMEM((beacons, rows, cols), F32),
            pltpu.VMEM((beacons, rows, cols), F32),
            pltpu.VMEM(blocks.shape, BF16),
            pltpu.VMEM((SIDE * CELLS, CELLS), BF16),
            pltpu.VMEM((beacons * rows, SIDE * CELLS), BF16),
            pltpu.VMEM((beacons * rows, CELLS), BF16),
            pltpu.VMEM((n, 1, n), jnp.int32),
            pltpu.VMEM((n, 1, n), jnp.int32),
            pltpu.VMEM((8, n), jnp.int32),
            pltpu.SMEM((8, n), jnp.int32),
            pltpu.VMEM((n * SIDE, n), F32),
            pltpu.VMEM((groups, beacons * n, GROUP * SIDE), BF16),
            pltpu.VMEM((n, SIDE, CELLS), BF16),
            pltpu.VMEM((n, SIDE, CELLS), BF16),
            pltpu.VMEM((n, SIDE, CELLS), BF16),
            pltpu.VMEM((n, SIDE, CELLS), BF16),
            pltpu.VMEM((beacons * rows, CELLS), F32),
            pltpu.VMEM((beacons * rows, CELLS), F32),
            pltpu.VMEM((4, 8, cols), F32),
            pltpu.VMEM((4, 8, cols), F32),
            pltpu.VMEM((1, 1, n), F32),
            pltpu.VMEM((n, 1, n), F32),
            dma((2,)),
            dma,
            dma,
            dma((2,)),
            dma((4,)),
            dma((4,)),
            dma,
            dma((groups,)),
            dma,
            dma((groups,)),
            dma((2,)),
        ],
        compiler_params=pltpu.CompilerParams(
            collective_id=0, has_side_effects=True, vmem_limit_bytes=60 * 1024 * 1024
        ),
        name="exchange",
    )(bin_owner.reshape(1, count), bin_tile.reshape(1, count), direction, residual, blocks)
    alpha = coef[0, :beacons, None, None]
    beta = coef[1, :beacons, None, None]
    next_residual = residual - alpha * image
    return solution + alpha * direction, next_residual, next_residual + beta * direction


def solution(mesh):
    field = P(None, "tx", "ty")
    placed = (field, field, field, P(("tx", "ty"), None, None), P(("tx", "ty"), None), P(("tx", "ty")))
    return jax.shard_map(
        functools.partial(per_device, mesh.shape["tx"], mesh.shape["ty"]),
        mesh=mesh,
        in_specs=placed,
        out_specs=(field, field, field),
        check_vma=False,
    )
```
